32 devices in a mesh: ep: 16 (over z, x, core), tp: 2 (over y).
Axes of the slice: x: 2, y: 2, z: 4, core: 2. Of those that a mesh axis runs over, the one named last changes fastest.
Arguments:
- attn: bfloat16 [2048, 2048], P('ep', 'tp'), may hold values from -6 to 6
- o_weight: bfloat16 [2048, 2048], P('tp'), may hold values from -0.125 to 0.125
- residual: bfloat16 [2048, 2048], P(('ep', 'tp')), may hold values from -6 to 6
- norm_gain: float32 [2048], replicated, may hold values from 0.5 to 2
- routes: int32 [2048, 6], P('ep'), may hold values from 0 to 15, all different within a row; in each aligned block of 64 rows (0 to 63, 64 to 127, ...) at most 32 rows name the same one
- route_logits: float32 [2048, 6], P('ep'), may hold values from -6 to 6
- expert_in: bfloat16 [16, 2, 2048, 1408], P('ep', None, None, 'tp'), may hold values from -0.125 to 0.125
- expert_out: bfloat16 [16, 2048, 1408], P('ep', None, 'tp'), may hold values from -0.15625 to 0.15625
- shared_in: bfloat16 [2, 2048, 1408], P(None, None, 'tp'), may hold values from -0.125 to 0.125
- shared_out: bfloat16 [2048, 1408], P(None, 'tp'), may hold values from -0.15625 to 0.15625
Outputs:
- block_out: bfloat16 [2048, 2048], P(('ep', 'tp'))
The draws below stay inside these ranges and needn't reach their ends.
Inputs may be any that keep to these rules, and one draw needn't show every extreme that they name: `routes`: each row names 6 different experts. Within each aligned block of 64 rows (the rows of one device) no expert is named by more than 32 rows, a bound that some block reaches.
All inputs are finite; a program needn't handle non-finite values.
Results may differ from the reference program's by a relative error of at most 0.0058.
Values may be sent and summed in bfloat16 or wider, within the bound.
A program may use at most 192 MiB of HBM per device.

```python
import math
import jax
import jax.numpy as jnp
import numpy as np
from jax import lax

D = 2048
HD = 2048
FF = 1408
SFF = 1408
TOP = 6
EXPERTS = 16
TOK_DEV = 64
TOKENS = 2048
CAP = 32


def level_of(key, shape, split, low, high):
    factor_of = 1.0
    for position, parts in split:
        steps = jax.random.uniform(jax.random.fold_in(jax.random.fold_in(key, 6), position), (parts,), jnp.float32, low / len(split), high / len(split))
        factor_of = factor_of * jnp.repeat(jnp.exp(steps), shape[position] // parts).reshape((-1,) + (1,) * (len(shape) - 1 - position))
    return factor_of


def routed_block(key, own, number, rows, number_of, top, bound, skew):
    sequence = jax.random.permutation(key, number_of)
    heavy_load, ordinary = portions_of(number_of, rows * top, bound, skew, True), portions_of(number_of, rows * top, bound, skew, False)
    places = jnp.arange(number_of)

    def named(sizes, offset_by):
        used = int((sizes > 0).sum())
        fixed = max(1, used // 4)
        moved = fixed + (places - fixed + offset_by * (used - fixed)) % max(1, number_of - fixed)
        return jnp.zeros((number_of,), jnp.int32).at[sequence[jnp.where(places < fixed, places, moved)]].set(jnp.asarray(sizes, jnp.int32))

    sizes = jnp.where(number % 4 == 0, named(heavy_load, number // 4), named(ordinary, number - number // 4 - 1))
    mixed = jax.random.permutation(jax.random.fold_in(own, 3), number_of)
    donor, receiver = mixed[0:number_of // 2 * 2:2], mixed[1:number_of // 2 * 2:2]
    room = jnp.minimum(sizes[donor] - 1, bound - sizes[receiver]) // 2
    room = jnp.where((donor == sequence[0]) | (receiver == sequence[0]) | (sizes[receiver] == 0), 0, jnp.maximum(room, 0))
    moved = jax.random.randint(jax.random.fold_in(own, 4), (number_of // 2,), 0, 1 << 20) % (room + 1)
    sizes = sizes.at[donor].add(-moved).at[receiver].add(moved)
    members = jnp.searchsorted(jnp.cumsum(sizes), jnp.arange(rows * top), side="right").astype(jnp.int32)
    listing = members.reshape(top, rows).T
    listing = listing[jax.random.permutation(jax.random.fold_in(own, 1), rows)]
    offset_by = jax.random.randint(jax.random.fold_in(own, 2), (rows, 1), 0, top)
    return jnp.take_along_axis(listing, (jnp.arange(top)[None, :] + offset_by) % top, axis=1)


def portions_of(amount, total, most, slope, full):
    loads = [(1 << 20) // math.isqrt(rank ** slope) + 1 for rank in range(1, amount + 1)]
    largest = most if full else min(most, max(-(-total // amount), total * loads[0] // sum(loads)))
    least = 1 if total - largest >= amount - 1 else 0
    holding, spare = [largest] + [least] * (amount - 1), total - largest - least * (amount - 1)
    while spare > 0:
        candidates = [i for i in range(1, amount) if holding[i] < largest] or [i for i in range(1, amount) if holding[i] < most]
        pool, remaining = sum([loads[i] for i in candidates]), spare
        for i in candidates:
            addition = min(most - holding[i], max(1, remaining * loads[i] // pool), spare)
            holding[i] = holding[i] + addition
            spare = spare - addition
    return np.array(holding)


def scatter_about(rng, dims, scale, reach, shards=(), kind=jnp.bfloat16):
    result = scale * jax.random.normal(rng, dims, jnp.float32)
    if shards:
        result = result * level_of(rng, dims, shards, -0.22, 0.18)
    return jnp.clip(result, -reach, reach).astype(kind)


def setup_inputs(seed: int = 0) -> dict:
    keys = jax.random.split(jax.random.key(seed), 11)
    attn = scatter_about(keys[0], (TOKENS, HD), 1.0, 6.0, ((0, 16), (1, 2)))
    o_weight = scatter_about(keys[1], (HD, D), HD ** -0.5, 0.125, ((0, 2),))
    residual = scatter_about(keys[2], (TOKENS, D), 1.0, 6.0, ((0, 32),))
    norm_gain = jnp.clip(jax.random.uniform(keys[3], (D,), jnp.float32, 0.5, 2.0), 0.5, 2.0)
    routes_keys = jax.random.split(jax.random.fold_in(keys[4], 1), TOKENS // TOK_DEV)
    routes_turns = jax.random.permutation(jax.random.fold_in(keys[4], 3), TOKENS // TOK_DEV)
    routes = jax.vmap(lambda own, number: routed_block(jax.random.fold_in(keys[4], 2), own, number, TOK_DEV, EXPERTS, TOP, CAP, 2))(routes_keys, routes_turns).reshape((TOKENS, TOP))
    route_logits = scatter_about(keys[5], (TOKENS, TOP), 1.5, 6.0, ((0, 16),), jnp.float32)
    expert_in = scatter_about(keys[6], (EXPERTS, 2, D, FF), D ** -0.5, 0.125, ((0, 16), (3, 2)))
    expert_out = scatter_about(keys[7], (EXPERTS, D, FF), FF ** -0.5, 0.15625, ((0, 16), (2, 2)))
    shared_in = scatter_about(keys[8], (2, D, SFF), D ** -0.5, 0.125, ((2, 2),))
    shared_out = scatter_about(keys[9], (D, SFF), SFF ** -0.5, 0.15625, ((1, 2),))
    return dict(attn=attn, o_weight=o_weight, residual=residual, norm_gain=norm_gain, routes=routes, route_logits=route_logits, expert_in=expert_in, expert_out=expert_out, shared_in=shared_in, shared_out=shared_out)


def reference(attn, o_weight, residual, norm_gain, routes, route_logits, expert_in, expert_out, shared_in, shared_out):
    hidden = residual.astype(jnp.float32) + jnp.dot(attn, o_weight, preferred_element_type=jnp.float32)
    inv_norm = lax.rsqrt(lax.optimization_barrier(jnp.mean(hidden * hidden, axis=-1, keepdims=True)) + 1e-06)
    normed = (hidden * inv_norm * norm_gain).astype(jnp.bfloat16)
    sigmoids = jax.nn.sigmoid(route_logits)
    route_weight = 2.446 * sigmoids / lax.optimization_barrier(jnp.sum(sigmoids, axis=-1, keepdims=True))
    blocks = TOKENS // TOK_DEV
    flat_routes = routes.reshape(blocks, TOK_DEV * TOP)
    onehot = (flat_routes[:, :, None] == jnp.arange(EXPERTS, dtype=jnp.int32)[None, None, :]).astype(jnp.int32)
    ranks = lax.optimization_barrier(jnp.sum((jnp.cumsum(onehot, axis=1) - onehot) * onehot, axis=2))
    depth = blocks * CAP
    places = flat_routes * depth + jnp.arange(blocks, dtype=jnp.int32)[:, None] * CAP + ranks
    token_ids = jnp.repeat(jnp.arange(TOKENS, dtype=jnp.int32), TOP)
    slot_tokens = jnp.full((EXPERTS * depth,), TOKENS, jnp.int32).at[places.reshape(-1)].set(token_ids)
    slot_weights = jnp.zeros((EXPERTS * depth,), jnp.float32).at[places.reshape(-1)].set(route_weight.reshape(-1))
    padded = jnp.concatenate([normed, jnp.zeros((1, D), jnp.bfloat16)], axis=0)

    def one_expert(accumulated, item):
        token_index, slot_scale, w_in, w_out = item
        chosen = padded[token_index]
        gate_val = jnp.dot(chosen, w_in[0], preferred_element_type=jnp.float32)
        up_val = jnp.dot(chosen, w_in[1], preferred_element_type=jnp.float32)
        active = (jax.nn.silu(gate_val) * up_val).astype(jnp.bfloat16)
        values = jnp.dot(active, w_out.T, preferred_element_type=jnp.float32)
        return (accumulated.at[token_index].add(slot_scale[:, None] * values), None)
    start_total = jnp.zeros((TOKENS + 1, D), jnp.float32)
    accumulated, unused = lax.scan(one_expert, start_total, (slot_tokens.reshape(EXPERTS, depth), slot_weights.reshape(EXPERTS, depth), expert_in, expert_out))
    shared_gate = jnp.dot(normed, shared_in[0], preferred_element_type=jnp.float32)
    shared_up = jnp.dot(normed, shared_in[1], preferred_element_type=jnp.float32)
    shared_act = (jax.nn.silu(shared_gate) * shared_up).astype(jnp.bfloat16)
    shared_val = jnp.dot(shared_act, shared_out.T, preferred_element_type=jnp.float32)
    return (hidden + accumulated[:TOKENS] + shared_val).astype(jnp.bfloat16)
```

```python
import jax
import jax.numpy as jnp
from jax import lax
from jax.experimental import pallas as pl
from jax.experimental.pallas import tpu as pltpu
from jax.sharding import PartitionSpec as P

PIECES = 4
PIECE_ROWS = 16
TRACKS = (
    (0, 640, "zxy"),
    (640, 640, "zyx"),
    (1280, 384, "xzy"),
    (1664, 384, "yzx"),
)
HIDDEN_TILES = 256
OUT_TILES = 256


def slot_places(route_rows, capacity, experts):
    flat_routes = route_rows.reshape(-1)
    onehot = (flat_routes[:, None] == jnp.arange(experts, dtype=jnp.int32)[None, :]).astype(
        jnp.int32
    )
    before = jnp.cumsum(onehot, axis=0) - onehot
    ranks = jnp.sum(before * onehot, axis=1)
    return flat_routes * capacity + ranks


def fill_slots(source_rows, places, capacity, experts, topk):
    copies = jnp.repeat(source_rows, topk, axis=0)
    empty_slots = jnp.zeros((experts * capacity, source_rows.shape[1]), source_rows.dtype)
    return empty_slots.at[places].set(copies)


def route_weights(logits):
    sigmoids = jax.nn.sigmoid(logits)
    return 2.446 * sigmoids / jnp.sum(sigmoids, axis=-1, keepdims=True)


def expert_part(slots, w_in, w_out):
    gate_val = jnp.einsum("slcd,ldf->slcf", slots, w_in[:, 0], preferred_element_type=jnp.float32)
    up_val = jnp.einsum("slcd,ldf->slcf", slots, w_in[:, 1], preferred_element_type=jnp.float32)
    active = (jax.nn.silu(gate_val) * up_val).astype(jnp.bfloat16)
    return jnp.einsum("slcf,ldf->slcd", active, w_out, preferred_element_type=jnp.float32)


def shared_part(source_rows, s_in, s_out):
    gate_val = jnp.dot(source_rows, s_in[0], preferred_element_type=jnp.float32)
    up_val = jnp.dot(source_rows, s_in[1], preferred_element_type=jnp.float32)
    active = (jax.nn.silu(gate_val) * up_val).astype(jnp.bfloat16)
    return jnp.einsum("tf,df->td", active, s_out, preferred_element_type=jnp.float32)


def combine_slots(values, places, weights, topk):
    picked = values[places].reshape(-1, topk, values.shape[1])
    return jnp.sum(picked * weights[:, :, None], axis=1)


def slotted_shards(
    attn,
    o_weight,
    residual,
    norm_gain,
    routes,
    route_logits,
    expert_in,
    expert_out,
    shared_in,
    shared_out,
):
    tok_rows = residual.shape[0]
    width = residual.shape[1]
    topk = routes.shape[1]
    tp_count = lax.axis_size("tp")
    ep_count = lax.axis_size("ep")
    local_experts = expert_in.shape[0]
    experts = local_experts * ep_count
    capacity = max(2, (4 * tok_rows * topk + 3 * experts - 1) // (3 * experts))
    attn_out = lax.psum_scatter(
        jnp.dot(attn, o_weight, preferred_element_type=jnp.float32),
        "tp",
        scatter_dimension=0,
        tiled=True,
    )
    hidden = residual.astype(jnp.float32) + attn_out
    inv_norm = lax.rsqrt(jnp.mean(hidden * hidden, axis=-1, keepdims=True) + 1e-06)
    normed = (hidden * inv_norm * norm_gain).astype(jnp.bfloat16)
    group_rows = lax.all_gather(normed, "tp", axis=0, tiled=True)
    group_cap = tp_count * capacity
    places = slot_places(routes, group_cap, experts)
    outgoing = fill_slots(group_rows, places, group_cap, experts, topk)
    incoming = lax.all_to_all(outgoing, "ep", split_axis=0, concat_axis=0, tiled=True)
    partial_value = expert_part(
        incoming.reshape(ep_count, local_experts, group_cap, width), expert_in, expert_out
    )
    returned = lax.all_to_all(
        partial_value.reshape(-1, width), "ep", split_axis=0, concat_axis=0, tiled=True
    )
    mixture = combine_slots(returned, places, route_weights(route_logits), topk)
    mixture = mixture + shared_part(group_rows, shared_in, shared_out)
    moe_sum = lax.psum_scatter(mixture, "tp", scatter_dimension=0, tiled=True)
    return (hidden + moe_sum).astype(jnp.bfloat16)


def place():
    ep = lax.axis_index("ep")
    return lax.div(ep, 4), lax.rem(lax.div(ep, 2), 2), lax.rem(ep, 2), lax.axis_index("tp")


def device_at(z, x, core, y):
    return (z * 4 + x * 2 + core, y)


def peers(z, x, core, y):
    along_z = [device_at(lax.rem(z + step, 4), x, core, y) for step in (1, 2, 3)]
    return (
        along_z,
        device_at(z, 1 - x, core, y),
        device_at(z, x, 1 - core, y),
        device_at(z, x, core, 1 - y),
    )


def remote(src, dst, send_sem, recv_sem, peer):
    return pltpu.make_async_remote_copy(
        src_ref=src,
        dst_ref=dst,
        send_sem=send_sem,
        recv_sem=recv_sem,
        device_id=peer,
        device_id_type=pl.DeviceIdType.MESH,
    )


def tiles(total, step):
    return [(start, min(step, total - start)) for start in range(0, total, step)]


def fused_kernel(
    attn_ref,
    gain_ref,
    residual_ref,
    w_ref,
    o_hbm,
    ein_hbm,
    eout_hbm,
    sin_hbm,
    sout_hbm,
    out_ref,
    o_vmem,
    ein,
    eout,
    s_in,
    s_out,
    products,
    hidden,
    away,
    arrived,
    rows_all,
    partial,
    core_in,
    w_all,
    w_cols,
    active,
    shared_active,
    shared_sum,
    *rest,
):
    boxes = rest[: 3 * len(TRACKS)]
    (
        load_sem,
        w_send,
        w_recv,
        y_send,
        y_recv,
        g_send,
        g_recv,
        gc_send,
        gc_recv,
        s_send,
        s_recv,
        sc_send,
        sc_recv,
    ) = rest[3 * len(TRACKS) :]
    f32, bf16 = jnp.float32, jnp.bfloat16
    z, x, core, y = place()
    along_z, x_peer, core_peer, y_peer = peers(z, x, core, y)
    ep = lax.axis_index("ep")
    mine = {"z": z, "x": x, "y": y}
    width = out_ref.shape[1]
    half = out_ref.shape[0]
    piece_total = 32 * PIECE_ROWS

    o_tiles = tiles(width, 512)
    o_loads = [
        pltpu.make_async_copy(
            o_hbm.at[:, pl.ds(start, size)], o_vmem.at[:, pl.ds(start, size)], load_sem.at[i]
        )
        for i, (start, size) in enumerate(o_tiles)
    ]
    weight_loads = [
        pltpu.make_async_copy(src, dst, load_sem.at[len(o_tiles) + i])
        for i, (src, dst) in enumerate(
            ((sin_hbm, s_in), (sout_hbm, s_out), (ein_hbm.at[0], ein), (eout_hbm.at[0], eout))
        )
    ]
    for copy in o_loads:
        copy.start()

    others = [lax.rem(ep + step, 16) for step in range(1, 16)]
    barrier = pltpu.get_barrier_semaphore()
    for peer in [(other, y) for other in others] + [y_peer]:
        pl.semaphore_signal(barrier, inc=1, device_id=peer, device_id_type=pl.DeviceIdType.MESH)

    for i, (start, size) in enumerate(o_tiles):
        o_loads[i].wait()
        products[:, start : start + size] = jnp.dot(
            attn_ref[...], o_vmem[:, start : start + size], preferred_element_type=f32
        )
    for copy in weight_loads:
        copy.start()
    for q in range(PIECES):
        away[q] = products[pl.ds((1 - y) * half + q * PIECE_ROWS, PIECE_ROWS), :].astype(bf16)

    pl.semaphore_wait(barrier, 16)

    def y_copy(q):
        return remote(away.at[q], arrived.at[q], y_send.at[q], y_recv.at[q], y_peer)

    for q in range(PIECES):
        y_copy(q).start()
    w_copies = [
        remote(w_ref.at[other], w_all.at[ep], w_send.at[i], w_recv.at[i], (other, y))
        for i, other in enumerate(others)
    ]
    for copy in w_copies:
        copy.start()
    w_all[ep] = w_ref[ep]

    def block(ref, q, index, cols):
        return ref.at[q, index["z"], index["x"], core, index["y"], :, cols]

    every = {"z": pl.ds(0, 4), "x": pl.ds(0, 2), "y": pl.ds(0, 2)}

    def gather_copies(q, track, stage):
        start, size, order = TRACKS[track]
        done, axis = order[:stage], order[stage]
        index = {a: every[a] if a in done else mine[a] for a in "zxy"}
        part = block(rows_all, q, index, pl.ds(start, size))
        slot = track * 5 + stage + (2 if "z" in done else 0)
        targets = along_z if axis == "z" else [x_peer if axis == "x" else y_peer]
        return [
            remote(part, part, g_send.at[q, slot + i], g_recv.at[q, slot + i], target)
            for i, target in enumerate(targets)
        ]

    def gather_core(q):
        part = rows_all.at[q, :, :, core]
        return remote(part, part, gc_send.at[q], gc_recv.at[q], core_peer)

    def scatter_core(q):
        return remote(
            partial.at[q, :, :, 1 - core], core_in.at[q], sc_send.at[q], sc_recv.at[q], core_peer
        )

    def scatter_index(track, stage, value):
        order = TRACKS[track][2][::-1]
        index = {a: every[a] for a in order[stage + 1 :]}
        index.update({a: mine[a] for a in order[:stage]})
        index[order[stage]] = value
        return index

    def scatter_copies(q, track, stage):
        start, size, order = TRACKS[track]
        axis = order[2 - stage]
        box = boxes[3 * track + stage]
        slot = track * 5 + stage + (2 if "z" in order[3 - stage :] else 0)
        if axis == "z":
            targets = [(along_z[i], lax.rem(z + i + 1, 4), box.at[q, i]) for i in range(3)]
        else:
            targets = [(x_peer if axis == "x" else y_peer, 1 - mine[axis], box.at[q, 0])]
        return [
            remote(
                block(partial, q, scatter_index(track, stage, value), pl.ds(start, size)),
                dst,
                s_send.at[q, slot + i],
                s_recv.at[q, slot + i],
                target,
            )
            for i, (target, value, dst) in enumerate(targets)
        ]

    def start_gather(q):
        y_copy(q).wait_recv()
        at = pl.multiple_of(q * PIECE_ROWS, PIECE_ROWS)
        own = pl.multiple_of(y * half + q * PIECE_ROWS, PIECE_ROWS)
        total = residual_ref[pl.ds(at, PIECE_ROWS), :].astype(f32)
        total = total + (products[pl.ds(own, PIECE_ROWS), :] + arrived[q].astype(f32))
        hidden[pl.ds(at, PIECE_ROWS), :] = total
        inv_norm = lax.rsqrt(jnp.mean(total * total, axis=-1, keepdims=True) + 1e-06)
        rows_all[q, z, x, core, y] = (total * inv_norm * gain_ref[...]).astype(bf16)
        for track in range(len(TRACKS)):
            for copy in gather_copies(q, track, 0):
                copy.start()

    def step_gather(stage):
        def step(q):
            for track in range(len(TRACKS)):
                for copy in gather_copies(q, track, stage - 1):
                    copy.wait_recv()
                if stage < 3:
                    for copy in gather_copies(q, track, stage):
                        copy.start()
            if stage == 3:
                gather_core(q).start()

        return step

    def end_gather(q):
        gather_core(q).wait_recv()

    def gate_up(rows, w_in, start, size):
        gate = jnp.dot(rows, w_in[0, :, start : start + size], preferred_element_type=f32)
        up = jnp.dot(rows, w_in[1, :, start : start + size], preferred_element_type=f32)
        return jax.nn.silu(gate) * up

    def down(act, w_out, start, size):
        return lax.dot_general(
            act, w_out[start : start + size, :], (((1,), (1,)), ((), ())),
            preferred_element_type=f32,
        )

    hidden_tiles = tiles(ein.shape[2], HIDDEN_TILES)
    out_tiles = tiles(width, OUT_TILES)

    def expert_in_tile(i):
        def step(q):
            start, size = hidden_tiles[i]
            rows = rows_all[q].reshape(piece_total, width)
            value = gate_up(rows, ein, start, size) * w_cols[q][:, 0:1]
            active[:, start : start + size] = value.astype(bf16)

        return step

    def expert_out_tiles(chosen):
        def step(q):
            for start, size in chosen:
                value = down(active[...], eout, start, size).astype(bf16)
                partial[q, :, :, :, :, :, start : start + size] = value.reshape(
                    4, 2, 2, 2, PIECE_ROWS, size
                )

        return step

    def shared_rows(q):
        rows = rows_all[q, z, x, core].reshape(2 * PIECE_ROWS, width)
        for start, size in hidden_tiles:
            shared_active[:, start : start + size] = gate_up(rows, s_in, start, size).astype(bf16)
        for start, size in out_tiles:
            shared_sum[:, start : start + size] = down(shared_active[...], s_out, start, size)

    def start_scatter(q):
        own = partial[q, z, x, core].reshape(2 * PIECE_ROWS, width).astype(f32) + shared_sum[...]
        partial[q, z, x, core] = own.astype(bf16).reshape(2, PIECE_ROWS, width)
        scatter_core(q).start()

    def after_core(q):
        scatter_core(q).wait_recv()

        def add(i, carry):
            a, b, c = lax.div(i, 4), lax.rem(lax.div(i, 2), 2), lax.rem(i, 2)
            total = partial[q, a, b, core, c].astype(f32) + core_in[q, a, b, c].astype(f32)
            partial[q, a, b, core, c] = total.astype(bf16)
            return carry

        lax.fori_loop(0, 16, add, 0)
        for track in range(len(TRACKS)):
            for copy in scatter_copies(q, track, 0):
                copy.start()

    def after_stage(stage):
        def step(q):
            for track in range(len(TRACKS)):
                start, size, order = TRACKS[track]
                cols = pl.ds(start, size)
                axis = order[2 - stage]
                left = [a for a in "zxy" if a in order[: 2 - stage]]
                box = boxes[3 * track + stage]
                for copy in scatter_copies(q, track, stage):
                    copy.wait_recv()
                counts = [4 if a == "z" else 2 for a in left]
                number = 1
                for count in counts:
                    number = number * count

                def add(i, carry):
                    index = dict(mine)
                    inner = []
                    rest_of = i
                    for a, count in reversed(list(zip(left, counts))):
                        index[a] = lax.rem(rest_of, count)
                        rest_of = lax.div(rest_of, count)
                        inner.insert(0, index[a])
                    at = (q, index["z"], index["x"], core, index["y"], slice(None), cols)
                    total = partial[at].astype(f32)
                    for j in range(3 if axis == "z" else 1):
                        total = total + box[(q, j, *inner)].astype(f32)
                    if stage == 2:
                        rows = pl.ds(pl.multiple_of(q * PIECE_ROWS, PIECE_ROWS), PIECE_ROWS)
                        out_ref[rows, cols] = (hidden[rows, cols] + total).astype(bf16)
                    else:
                        partial[at] = total.astype(bf16)
                    return carry

                if number == 1:
                    add(0, 0)
                else:
                    lax.fori_loop(0, number, add, 0)
                if stage < 2:
                    for copy in scatter_copies(q, track, stage + 1):
                        copy.start()

        return step

    start_gather(0)
    start_gather(1)

    for copy in w_copies:
        copy.wait_recv()
    turned = jnp.transpose(w_all[...].reshape(128, 128))
    for q in range(PIECES):
        for e in range(16):
            for b in range(2):
                at = e * 2 * PIECE_ROWS + b * PIECE_ROWS
                source = b * half + q * PIECE_ROWS
                w_cols[q, at : at + PIECE_ROWS, :] = jnp.broadcast_to(
                    turned[source : source + PIECE_ROWS, e * 8 : e * 8 + 1], (PIECE_ROWS, 128)
                )
    for copy in weight_loads:
        copy.wait()

    middle = len(out_tiles) // 2
    plan = [
        (-3, end_gather),
        (-3, expert_in_tile(0)),
        (-4, after_core),
        (-3, expert_in_tile(1)),
        (0, step_gather(1)),
        (2, start_gather),
        (-3, expert_in_tile(2)),
        (-1, step_gather(2)),
        (-3, expert_out_tiles(out_tiles[:middle])),
        (-5, after_stage(0)),
        (-2, step_gather(3)),
        (-3, expert_out_tiles(out_tiles[middle:])),
        (-3, start_scatter),
        (-6, after_stage(1)),
        (-7, after_stage(2)),
        (-2, shared_rows),
    ]
    turns = PIECES - min(shift for shift, _ in plan)

    def turn(u, carry):
        for shift, step in plan:
            q = u + shift

            @pl.when(jnp.logical_and(q >= 0, q < PIECES))
            def run(step=step, q=q):
                step(q)

        return carry

    lax.fori_loop(0, turns, turn, 0)

    def finish(q, carry):
        y_copy(q).wait_send()
        gather_core(q).wait_send()
        scatter_core(q).wait_send()
        for track in range(len(TRACKS)):
            for stage in range(3):
                for copy in gather_copies(q, track, stage) + scatter_copies(q, track, stage):
                    copy.wait_send()
        return carry

    lax.fori_loop(0, PIECES, finish, 0)
    for copy in w_copies:
        copy.wait_send()


def fused(attn, gain, residual, weights, o_weight, expert_in, expert_out, shared_in, shared_out):
    rows, width = residual.shape
    hidden_units = expert_in.shape[3]
    bf16, f32 = jnp.bfloat16, jnp.float32
    boxes = []
    for _, size, order in TRACKS:
        for stage in range(3):
            left = [4 if a == "z" else 2 for a in "zxy" if a in order[: 2 - stage]]
            boxes.append(
                pltpu.VMEM(
                    (PIECES, 3 if order[2 - stage] == "z" else 1, *left, PIECE_ROWS, size), bf16
                )
            )
    dma = pltpu.SemaphoreType.DMA
    slots = 5 * len(TRACKS)
    vmem = pl.BlockSpec(memory_space=pltpu.VMEM)
    hbm = pl.BlockSpec(memory_space=pl.ANY)
    return pl.pallas_call(
        fused_kernel,
        out_shape=jax.ShapeDtypeStruct((rows, width), bf16),
        in_specs=[vmem] * 4 + [hbm] * 5,
        out_specs=vmem,
        scratch_shapes=[
            pltpu.VMEM(o_weight.shape, bf16),
            pltpu.VMEM(expert_in.shape[1:], bf16),
            pltpu.VMEM(expert_out.shape[1:], bf16),
            pltpu.VMEM(shared_in.shape, bf16),
            pltpu.VMEM(shared_out.shape, bf16),
            pltpu.VMEM((2 * rows, width), f32),
            pltpu.VMEM((rows, width), f32),
            pltpu.VMEM((PIECES, PIECE_ROWS, width), bf16),
            pltpu.VMEM((PIECES, PIECE_ROWS, width), bf16),
            pltpu.VMEM((PIECES, 4, 2, 2, 2, PIECE_ROWS, width), bf16),
            pltpu.VMEM((PIECES, 4, 2, 2, 2, PIECE_ROWS, width), bf16),
            pltpu.VMEM((PIECES, 4, 2, 2, PIECE_ROWS, width), bf16),
            pltpu.VMEM((16, 8, 128), f32),
            pltpu.VMEM((PIECES, 32 * PIECE_ROWS, 128), f32),
            pltpu.VMEM((32 * PIECE_ROWS, hidden_units), bf16),
            pltpu.VMEM((2 * PIECE_ROWS, hidden_units), bf16),
            pltpu.VMEM((2 * PIECE_ROWS, width), f32),
            *boxes,
            dma((8,)),
            dma((15,)),
            dma((15,)),
            dma((PIECES,)),
            dma((PIECES,)),
            dma((PIECES, slots)),
            dma((PIECES, slots)),
            dma((PIECES,)),
            dma((PIECES,)),
            dma((PIECES, slots)),
            dma((PIECES, slots)),
            dma((PIECES,)),
            dma((PIECES,)),
        ],
        compiler_params=pltpu.CompilerParams(
            collective_id=0, has_side_effects=True, vmem_limit_bytes=60 * 1024 * 1024
        ),
    )(attn, gain, residual, weights, o_weight, expert_in, expert_out, shared_in, shared_out)


def fused_shards(
    attn,
    o_weight,
    residual,
    norm_gain,
    routes,
    route_logits,
    expert_in,
    expert_out,
    shared_in,
    shared_out,
):
    experts = expert_in.shape[0] * lax.axis_size("ep")
    weights = route_weights(route_logits)
    chosen = routes[:, :, None] == jnp.arange(experts, dtype=jnp.int32)[None, None, :]
    dense_weights = jnp.sum(jnp.where(chosen, weights[:, :, None], 0.0), axis=1)
    out_weights = jnp.broadcast_to(dense_weights.T[:, None, :], (experts, 8, routes.shape[0]))
    return fused(
        attn,
        norm_gain[None, :],
        residual,
        out_weights,
        o_weight,
        expert_in,
        expert_out,
        shared_in,
        shared_out,
    )


def shards(*args):
    routes, expert_in = args[4], args[6]
    experts = expert_in.shape[0] * lax.axis_size("ep")
    spans = lax.axis_size("ep") == 16 and lax.axis_size("tp") == 2
    fits = args[2].shape[0] == PIECES * PIECE_ROWS and expert_in.shape[0] == 1
    if spans and fits and experts <= 4 * routes.shape[1]:
        return fused_shards(*args)
    return slotted_shards(*args)


def solution(mesh):
    in_specs = (
        P("ep", "tp"),
        P("tp", None),
        P(("ep", "tp"), None),
        P(),
        P("ep", None),
        P("ep", None),
        P("ep", None, None, "tp"),
        P("ep", None, "tp"),
        P(None, None, "tp"),
        P(None, "tp"),
    )
    out_specs = P(("ep", "tp"), None)
    return jax.shard_map(shards, mesh=mesh, in_specs=in_specs, out_specs=out_specs, check_vma=False)
```

```python
import jax
import jax.numpy as jnp
from jax import lax
from jax.experimental import pallas as pl
from jax.experimental.pallas import tpu as pltpu
from jax.sharding import PartitionSpec as P

PIECES = 4
PIECE_ROWS = 16
TRACKS = (
    (0, 640, "zxy"),
    (640, 640, "zyx"),
    (1280, 384, "xzy"),
    (1664, 384, "yzx"),
)
HIDDEN_TILES = 256
OUT_TILES = 256


def slot_places(route_rows, capacity, experts):
    flat_routes = route_rows.reshape(-1)
    onehot = (flat_routes[:, None] == jnp.arange(experts, dtype=jnp.int32)[None, :]).astype(
        jnp.int32
    )
    before = jnp.cumsum(onehot, axis=0) - onehot
    ranks = jnp.sum(before * onehot, axis=1)
    return flat_routes * capacity + ranks


def fill_slots(source_rows, places, capacity, experts, topk):
    copies = jnp.repeat(source_rows, topk, axis=0)
    empty_slots = jnp.zeros((experts * capacity, source_rows.shape[1]), source_rows.dtype)
    return empty_slots.at[places].set(copies)


def route_weights(logits):
    sigmoids = jax.nn.sigmoid(logits)
    return 2.446 * sigmoids / jnp.sum(sigmoids, axis=-1, keepdims=True)


def expert_part(slots, w_in, w_out):
    gate_val = jnp.einsum("slcd,ldf->slcf", slots, w_in[:, 0], preferred_element_type=jnp.float32)
    up_val = jnp.einsum("slcd,ldf->slcf", slots, w_in[:, 1], preferred_element_type=jnp.float32)
    active = (jax.nn.silu(gate_val) * up_val).astype(jnp.bfloat16)
    return jnp.einsum("slcf,ldf->slcd", active, w_out, preferred_element_type=jnp.float32)


def shared_part(source_rows, s_in, s_out):
    gate_val = jnp.dot(source_rows, s_in[0], preferred_element_type=jnp.float32)
    up_val = jnp.dot(source_rows, s_in[1], preferred_element_type=jnp.float32)
    active = (jax.nn.silu(gate_val) * up_val).astype(jnp.bfloat16)
    return jnp.einsum("tf,df->td", active, s_out, preferred_element_type=jnp.float32)


def combine_slots(values, places, weights, topk):
    picked = values[places].reshape(-1, topk, values.shape[1])
    return jnp.sum(picked * weights[:, :, None], axis=1)


def slotted_shards(
    attn,
    o_weight,
    residual,
    norm_gain,
    routes,
    route_logits,
    expert_in,
    expert_out,
    shared_in,
    shared_out,
):
    tok_rows = residual.shape[0]
    width = residual.shape[1]
    topk = routes.shape[1]
    tp_count = lax.axis_size("tp")
    ep_count = lax.axis_size("ep")
    local_experts = expert_in.shape[0]
    experts = local_experts * ep_count
    capacity = max(2, (4 * tok_rows * topk + 3 * experts - 1) // (3 * experts))
    attn_out = lax.psum_scatter(
        jnp.dot(attn, o_weight, preferred_element_type=jnp.float32),
        "tp",
        scatter_dimension=0,
        tiled=True,
    )
    hidden = residual.astype(jnp.float32) + attn_out
    inv_norm = lax.rsqrt(jnp.mean(hidden * hidden, axis=-1, keepdims=True) + 1e-06)
    normed = (hidden * inv_norm * norm_gain).astype(jnp.bfloat16)
    group_rows = lax.all_gather(normed, "tp", axis=0, tiled=True)
    group_cap = tp_count * capacity
    places = slot_places(routes, group_cap, experts)
    outgoing = fill_slots(group_rows, places, group_cap, experts, topk)
    incoming = lax.all_to_all(outgoing, "ep", split_axis=0, concat_axis=0, tiled=True)
    partial_value = expert_part(
        incoming.reshape(ep_count, local_experts, group_cap, width), expert_in, expert_out
    )
    returned = lax.all_to_all(
        partial_value.reshape(-1, width), "ep", split_axis=0, concat_axis=0, tiled=True
    )
    mixture = combine_slots(returned, places, route_weights(route_logits), topk)
    mixture = mixture + shared_part(group_rows, shared_in, shared_out)
    moe_sum = lax.psum_scatter(mixture, "tp", scatter_dimension=0, tiled=True)
    return (hidden + moe_sum).astype(jnp.bfloat16)


def place():
    ep = lax.axis_index("ep")
    return lax.div(ep, 4), lax.rem(lax.div(ep, 2), 2), lax.rem(ep, 2), lax.axis_index("tp")


def device_at(z, x, core, y):
    return (z * 4 + x * 2 + core, y)


def peers(z, x, core, y):
    along_z = [device_at(lax.rem(z + step, 4), x, core, y) for step in (1, 2, 3)]
    return (
        along_z,
        device_at(z, 1 - x, core, y),
        device_at(z, x, 1 - core, y),
        device_at(z, x, core, 1 - y),
    )


def remote(src, dst, send_sem, recv_sem, peer):
    return pltpu.make_async_remote_copy(
        src_ref=src,
        dst_ref=dst,
        send_sem=send_sem,
        recv_sem=recv_sem,
        device_id=peer,
        device_id_type=pl.DeviceIdType.MESH,
    )


def tiles(total, step):
    return [(start, min(step, total - start)) for start in range(0, total, step)]


def fused_kernel(
    attn_ref,
    gain_ref,
    residual_ref,
    routes_ref,
    logits_ref,
    o_hbm,
    ein_hbm,
    eout_hbm,
    sin_hbm,
    sout_hbm,
    out_ref,
    o_vmem,
    ein,
    eout,
    s_in,
    s_out,
    products,
    hidden,
    away,
    arrived,
    rows_all,
    partial,
    core_in,
    w_mine,
    w_all,
    w_cols,
    active,
    shared_active,
    shared_sum,
    *rest,
):
    boxes = rest[: 3 * len(TRACKS)]
    (
        load_sem,
        w_send,
        w_recv,
        y_send,
        y_recv,
        g_send,
        g_recv,
        gc_send,
        gc_recv,
        s_send,
        s_recv,
        sc_send,
        sc_recv,
    ) = rest[3 * len(TRACKS) :]
    f32, bf16 = jnp.float32, jnp.bfloat16
    z, x, core, y = place()
    along_z, x_peer, core_peer, y_peer = peers(z, x, core, y)
    ep = lax.axis_index("ep")
    mine = {"z": z, "x": x, "y": y}
    width = out_ref.shape[1]
    half = out_ref.shape[0]
    piece_total = 32 * PIECE_ROWS

    o_tiles = tiles(width, 512)
    o_loads = [
        pltpu.make_async_copy(
            o_hbm.at[:, pl.ds(start, size)], o_vmem.at[:, pl.ds(start, size)], load_sem.at[i]
        )
        for i, (start, size) in enumerate(o_tiles)
    ]
    weight_loads = [
        pltpu.make_async_copy(src, dst, load_sem.at[len(o_tiles) + i])
        for i, (src, dst) in enumerate(
            ((sin_hbm, s_in), (sout_hbm, s_out), (ein_hbm.at[0], ein), (eout_hbm.at[0], eout))
        )
    ]
    for copy in o_loads:
        copy.start()

    others = [lax.rem(ep + step, 16) for step in range(1, 16)]
    barrier = pltpu.get_barrier_semaphore()
    for peer in [(other, y) for other in others] + [y_peer]:
        pl.semaphore_signal(barrier, inc=1, device_id=peer, device_id_type=pl.DeviceIdType.MESH)

    sigmoids = jax.nn.sigmoid(logits_ref[...])
    weights = 2.446 * sigmoids / jnp.sum(sigmoids, axis=0, keepdims=True)
    for e in range(16):
        named = jnp.where(routes_ref[...] == e, weights, 0.0)
        w_mine[e] = jnp.broadcast_to(jnp.sum(named, axis=0, keepdims=True), (8, 128))

    for i, (start, size) in enumerate(o_tiles):
        o_loads[i].wait()
        products[:, start : start + size] = jnp.dot(
            attn_ref[...], o_vmem[:, start : start + size], preferred_element_type=f32
        )
    for copy in weight_loads:
        copy.start()
    for q in range(PIECES):
        away[q] = products[pl.ds((1 - y) * half + q * PIECE_ROWS, PIECE_ROWS), :].astype(bf16)

    pl.semaphore_wait(barrier, 16)

    def y_copy(q):
        return remote(away.at[q], arrived.at[q], y_send.at[q], y_recv.at[q], y_peer)

    for q in range(PIECES):
        y_copy(q).start()
    w_copies = [
        remote(w_mine.at[other], w_all.at[ep], w_send.at[i], w_recv.at[i], (other, y))
        for i, other in enumerate(others)
    ]
    for copy in w_copies:
        copy.start()
    w_all[ep] = w_mine[ep]

    def block(ref, q, index, cols):
        return ref.at[q, index["z"], index["x"], core, index["y"], :, cols]

    every = {"z": pl.ds(0, 4), "x": pl.ds(0, 2), "y": pl.ds(0, 2)}

    def gather_copies(q, track, stage):
        start, size, order = TRACKS[track]
        done, axis = order[:stage], order[stage]
        index = {a: every[a] if a in done else mine[a] for a in "zxy"}
        part = block(rows_all, q, index, pl.ds(start, size))
        slot = track * 5 + stage + (2 if "z" in done else 0)
        targets = along_z if axis == "z" else [x_peer if axis == "x" else y_peer]
        return [
            remote(part, part, g_send.at[q, slot + i], g_recv.at[q, slot + i], target)
            for i, target in enumerate(targets)
        ]

    def gather_core(q):
        part = rows_all.at[q, :, :, core]
        return remote(part, part, gc_send.at[q], gc_recv.at[q], core_peer)

    def scatter_core(q):
        return remote(
            partial.at[q, :, :, 1 - core], core_in.at[q], sc_send.at[q], sc_recv.at[q], core_peer
        )

    def scatter_index(track, stage, value):
        order = TRACKS[track][2][::-1]
        index = {a: every[a] for a in order[stage + 1 :]}
        index.update({a: mine[a] for a in order[:stage]})
        index[order[stage]] = value
        return index

    def scatter_copies(q, track, stage):
        start, size, order = TRACKS[track]
        axis = order[2 - stage]
        box = boxes[3 * track + stage]
        slot = track * 5 + stage + (2 if "z" in order[3 - stage :] else 0)
        if axis == "z":
            targets = [(along_z[i], lax.rem(z + i + 1, 4), box.at[q, i]) for i in range(3)]
        else:
            targets = [(x_peer if axis == "x" else y_peer, 1 - mine[axis], box.at[q, 0])]
        return [
            remote(
                block(partial, q, scatter_index(track, stage, value), pl.ds(start, size)),
                dst,
                s_send.at[q, slot + i],
                s_recv.at[q, slot + i],
                target,
            )
            for i, (target, value, dst) in enumerate(targets)
        ]

    def start_gather(q):
        y_copy(q).wait_recv()
        at = pl.multiple_of(q * PIECE_ROWS, PIECE_ROWS)
        own = pl.multiple_of(y * half + q * PIECE_ROWS, PIECE_ROWS)
        total = residual_ref[pl.ds(at, PIECE_ROWS), :].astype(f32)
        total = total + (products[pl.ds(own, PIECE_ROWS), :] + arrived[q].astype(f32))
        hidden[pl.ds(at, PIECE_ROWS), :] = total
        inv_norm = lax.rsqrt(jnp.mean(total * total, axis=-1, keepdims=True) + 1e-06)
        rows_all[q, z, x, core, y] = (total * inv_norm * gain_ref[...]).astype(bf16)
        for track in range(len(TRACKS)):
            for copy in gather_copies(q, track, 0):
                copy.start()

    def step_gather(stage):
        def step(q):
            for track in range(len(TRACKS)):
                for copy in gather_copies(q, track, stage - 1):
                    copy.wait_recv()
                if stage < 3:
                    for copy in gather_copies(q, track, stage):
                        copy.start()
            if stage == 3:
                gather_core(q).start()

        return step

    def end_gather(q):
        gather_core(q).wait_recv()

    def gate_up(rows, w_in, start, size):
        both = [
            lax.dot_general(
                rows, w_in[i, start : start + size, :], (((1,), (1,)), ((), ())),
                preferred_element_type=f32,
            )
            for i in range(2)
        ]
        return jax.nn.silu(both[0]) * both[1]

    def down(act, w_out, start, size):
        return jnp.dot(act, w_out[:, start : start + size], preferred_element_type=f32)

    hidden_tiles = tiles(ein.shape[1], HIDDEN_TILES)
    out_tiles = tiles(width, OUT_TILES)

    def expert_in_tile(i):
        def step(q):
            start, size = hidden_tiles[i]
            rows = rows_all[q].reshape(piece_total, width)
            value = gate_up(rows, ein, start, size) * w_cols[q][:, 0:1]
            active[:, start : start + size] = value.astype(bf16)

        return step

    def expert_out_tiles(chosen):
        def step(q):
            for start, size in chosen:
                value = down(active[...], eout, start, size).astype(bf16)
                partial[q, :, :, :, :, :, start : start + size] = value.reshape(
                    4, 2, 2, 2, PIECE_ROWS, size
                )

        return step

    def shared_rows(q):
        rows = rows_all[q, z, x, core].reshape(2 * PIECE_ROWS, width)
        for start, size in hidden_tiles:
            shared_active[:, start : start + size] = gate_up(rows, s_in, start, size).astype(bf16)
        for start, size in out_tiles:
            shared_sum[:, start : start + size] = down(shared_active[...], s_out, start, size)

    def start_scatter(q):
        own = partial[q, z, x, core].reshape(2 * PIECE_ROWS, width).astype(f32) + shared_sum[...]
        partial[q, z, x, core] = own.astype(bf16).reshape(2, PIECE_ROWS, width)
        scatter_core(q).start()

    def after_core(q):
        scatter_core(q).wait_recv()

        def add(i, carry):
            a, b, c = lax.div(i, 4), lax.rem(lax.div(i, 2), 2), lax.rem(i, 2)
            total = partial[q, a, b, core, c].astype(f32) + core_in[q, a, b, c].astype(f32)
            partial[q, a, b, core, c] = total.astype(bf16)
            return carry

        lax.fori_loop(0, 16, add, 0)
        for track in range(len(TRACKS)):
            for copy in scatter_copies(q, track, 0):
                copy.start()

    def after_stage(stage):
        def step(q):
            for track in range(len(TRACKS)):
                start, size, order = TRACKS[track]
                cols = pl.ds(start, size)
                axis = order[2 - stage]
                left = [a for a in "zxy" if a in order[: 2 - stage]]
                box = boxes[3 * track + stage]
                for copy in scatter_copies(q, track, stage):
                    copy.wait_recv()
                counts = [4 if a == "z" else 2 for a in left]
                number = 1
                for count in counts:
                    number = number * count

                def add(i, carry):
                    index = dict(mine)
                    inner = []
                    rest_of = i
                    for a, count in reversed(list(zip(left, counts))):
                        index[a] = lax.rem(rest_of, count)
                        rest_of = lax.div(rest_of, count)
                        inner.insert(0, index[a])
                    at = (q, index["z"], index["x"], core, index["y"], slice(None), cols)
                    total = partial[at].astype(f32)
                    for j in range(3 if axis == "z" else 1):
                        total = total + box[(q, j, *inner)].astype(f32)
                    if stage == 2:
                        rows = pl.ds(pl.multiple_of(q * PIECE_ROWS, PIECE_ROWS), PIECE_ROWS)
                        out_ref[rows, cols] = (hidden[rows, cols] + total).astype(bf16)
                    else:
                        partial[at] = total.astype(bf16)
                    return carry

                if number == 1:
                    add(0, 0)
                else:
                    lax.fori_loop(0, number, add, 0)
                if stage < 2:
                    for copy in scatter_copies(q, track, stage + 1):
                        copy.start()

        return step

    start_gather(0)
    start_gather(1)

    for copy in w_copies:
        copy.wait_recv()
    turned = jnp.transpose(w_all[...].reshape(128, 128))
    for q in range(PIECES):
        for e in range(16):
            for b in range(2):
                at = e * 2 * PIECE_ROWS + b * PIECE_ROWS
                source = b * half + q * PIECE_ROWS
                w_cols[q, at : at + PIECE_ROWS, :] = jnp.broadcast_to(
                    turned[source : source + PIECE_ROWS, e * 8 : e * 8 + 1], (PIECE_ROWS, 128)
                )
    for copy in weight_loads:
        copy.wait()

    middle = len(out_tiles) // 2
    plan = [
        (-3, end_gather),
        (-3, expert_in_tile(0)),
        (-4, after_core),
        (-3, expert_in_tile(1)),
        (0, step_gather(1)),
        (2, start_gather),
        (-3, expert_in_tile(2)),
        (-1, step_gather(2)),
        (-3, expert_out_tiles(out_tiles[:middle])),
        (-5, after_stage(0)),
        (-2, step_gather(3)),
        (-3, expert_out_tiles(out_tiles[middle:])),
        (-3, start_scatter),
        (-6, after_stage(1)),
        (-7, after_stage(2)),
        (-2, shared_rows),
    ]
    turns = PIECES - min(shift for shift, _ in plan)

    def turn(u, carry):
        for shift, step in plan:
            q = u + shift

            @pl.when(jnp.logical_and(q >= 0, q < PIECES))
            def run(step=step, q=q):
                step(q)

        return carry

    lax.fori_loop(0, turns, turn, 0)

    def finish(q, carry):
        y_copy(q).wait_send()
        gather_core(q).wait_send()
        scatter_core(q).wait_send()
        for track in range(len(TRACKS)):
            for stage in range(3):
                for copy in gather_copies(q, track, stage) + scatter_copies(q, track, stage):
                    copy.wait_send()
        return carry

    lax.fori_loop(0, PIECES, finish, 0)
    for copy in w_copies:
        copy.wait_send()


def fused(
    attn, gain, residual, routes, logits, o_weight, expert_in, expert_out, shared_in, shared_out
):
    rows, width = residual.shape
    hidden_units = expert_in.shape[2]
    bf16, f32 = jnp.bfloat16, jnp.float32
    boxes = []
    for _, size, order in TRACKS:
        for stage in range(3):
            left = [4 if a == "z" else 2 for a in "zxy" if a in order[: 2 - stage]]
            boxes.append(
                pltpu.VMEM(
                    (PIECES, 3 if order[2 - stage] == "z" else 1, *left, PIECE_ROWS, size), bf16
                )
            )
    dma = pltpu.SemaphoreType.DMA
    slots = 5 * len(TRACKS)
    vmem = pl.BlockSpec(memory_space=pltpu.VMEM)
    hbm = pl.BlockSpec(memory_space=pl.ANY)
    return pl.pallas_call(
        fused_kernel,
        out_shape=jax.ShapeDtypeStruct((rows, width), bf16),
        in_specs=[vmem] * 5 + [hbm] * 5,
        out_specs=vmem,
        scratch_shapes=[
            pltpu.VMEM(o_weight.shape, bf16),
            pltpu.VMEM(expert_in.shape[1:], bf16),
            pltpu.VMEM(expert_out.shape[1:], bf16),
            pltpu.VMEM(shared_in.shape, bf16),
            pltpu.VMEM(shared_out.shape, bf16),
            pltpu.VMEM((2 * rows, width), f32),
            pltpu.VMEM((rows, width), f32),
            pltpu.VMEM((PIECES, PIECE_ROWS, width), bf16),
            pltpu.VMEM((PIECES, PIECE_ROWS, width), bf16),
            pltpu.VMEM((PIECES, 4, 2, 2, 2, PIECE_ROWS, width), bf16),
            pltpu.VMEM((PIECES, 4, 2, 2, 2, PIECE_ROWS, width), bf16),
            pltpu.VMEM((PIECES, 4, 2, 2, PIECE_ROWS, width), bf16),
            pltpu.VMEM((16, 8, 128), f32),
            pltpu.VMEM((16, 8, 128), f32),
            pltpu.VMEM((PIECES, 32 * PIECE_ROWS, 128), f32),
            pltpu.VMEM((32 * PIECE_ROWS, hidden_units), bf16),
            pltpu.VMEM((2 * PIECE_ROWS, hidden_units), bf16),
            pltpu.VMEM((2 * PIECE_ROWS, width), f32),
            *boxes,
            dma((8,)),
            dma((15,)),
            dma((15,)),
            dma((PIECES,)),
            dma((PIECES,)),
            dma((PIECES, slots)),
            dma((PIECES, slots)),
            dma((PIECES,)),
            dma((PIECES,)),
            dma((PIECES, slots)),
            dma((PIECES, slots)),
            dma((PIECES,)),
            dma((PIECES,)),
        ],
        compiler_params=pltpu.CompilerParams(
            collective_id=0, has_side_effects=True, vmem_limit_bytes=60 * 1024 * 1024
        ),
    )(attn, gain, residual, routes, logits, o_weight, expert_in, expert_out, shared_in, shared_out)


def fused_shards(
    attn,
    o_weight,
    residual,
    norm_gain,
    routes,
    route_logits,
    expert_in,
    expert_out,
    shared_in,
    shared_out,
):
    return fused(
        attn,
        norm_gain[None, :],
        residual,
        routes.T,
        route_logits.T,
        o_weight,
        jnp.swapaxes(expert_in, 2, 3),
        jnp.swapaxes(expert_out, 1, 2),
        jnp.swapaxes(shared_in, 1, 2),
        shared_out.T,
    )


def shards(*args):
    routes, expert_in = args[4], args[6]
    experts = expert_in.shape[0] * lax.axis_size("ep")
    spans = lax.axis_size("ep") == 16 and lax.axis_size("tp") == 2
    fits = args[2].shape[0] == PIECES * PIECE_ROWS and expert_in.shape[0] == 1
    if spans and fits and experts <= 4 * routes.shape[1]:
        return fused_shards(*args)
    return slotted_shards(*args)


def solution(mesh):
    in_specs = (
        P("ep", "tp"),
        P("tp", None),
        P(("ep", "tp"), None),
        P(),
        P("ep", None),
        P("ep", None),
        P("ep", None, None, "tp"),
        P("ep", None, "tp"),
        P(None, None, "tp"),
        P(None, "tp"),
    )
    out_specs = P(("ep", "tp"), None)
    return jax.shard_map(shards, mesh=mesh, in_specs=in_specs, out_specs=out_specs, check_vma=False)
```
